32 devices in a mesh: dom: 8 (over z, y), head: 4 (over x, core).
Axes of the slice: x: 2, y: 2, z: 4, core: 2. Of those that a mesh axis runs over, the one named last changes fastest.
Arguments:
- node_feats: bfloat16 [4096, 1024], P('dom'), may hold values from -16 to 16
- block_list: int32 [32, 12], replicated, may hold values from 0 to 31, as said below
- w_query: bfloat16 [1024, 1024], P('dom', 'head'), may hold values from -0.1875 to 0.1875
- w_key: bfloat16 [1024, 1024], P('dom', 'head'), may hold values from -0.1875 to 0.1875
- w_value: bfloat16 [1024, 1024], P('dom', 'head'), may hold values from -0.1875 to 0.1875
- w_out: bfloat16 [1024, 1024], P('dom', 'head'), may hold values from -0.1875 to 0.1875
- cotangent: bfloat16 [4096, 1024], P('dom'), may hold values from -6 to 6
Outputs:
- mixed_out: bfloat16 [4096, 1024], P('dom', 'head')
- grad_feats: bfloat16 [4096, 1024], P('dom', 'head')
- grad_wq: float32 [1024, 1024], P('dom', 'head')
- grad_wk: float32 [1024, 1024], P('dom', 'head')
- grad_wv: float32 [1024, 1024], P('dom', 'head')
- grad_wo: float32 [1024, 1024], P('dom', 'head')
The draws below stay inside these ranges and needn't reach their ends.
Inputs may be any that keep to these rules, and one draw needn't show every extreme that they name: `block_list`: row b names first 3 distinct blocks of b's own partition p = b // 4 (blocks p * 4 to p * 4 + 3), then 9 blocks of other partitions, which may repeat. Over all rows of one partition, at most 2 distinct blocks of any one other partition are named, and in every draw some partition names exactly 2 blocks of another.
All inputs are finite; a program needn't handle non-finite values.
Results may differ from the reference program's by a relative error of at most 0.011.
The reference program's roundings to bfloat16 on the way count: a program that leaves them out, or rounds other values in their place, can miss the bound.
Values may be sent and summed in bfloat16 or wider, within the bound.
No kernel may reach another device: no remote copies, remote signals or barrier semaphores. Data moves between devices by JAX's collectives and lax.ppermute only.
A program may use at most 192 MiB of HBM per device.

```python
import jax
import jax.numpy as jnp
from jax import lax

MODEL_WIDTH = 1024
HEAD_COUNT = 16
HEAD_WIDTH = 64
BLOCK_NODES = 128
NLOC = 3
NEXP = 9
CAP = 2
NB_DEV = 4
SLOTS_PER_BLOCK = 12
BLOCKS = 32
NODES = 4096
N_HEAD = 4


def draw_node_feats(key, part):
    key_one = jax.random.fold_in(key, 0)
    result = jnp.clip(jax.random.normal(key_one, (NODES, MODEL_WIDTH), jnp.float32), -4.0, 4.0)
    return result.astype(jnp.bfloat16)


def draw_block_list(key, part):
    dom_count = BLOCKS // NB_DEV
    key_one, key_two, key_three, key_four = jax.random.split(key, 4)
    device = jnp.arange(BLOCKS) // NB_DEV
    local_scores = jax.random.randint(key_one, (BLOCKS, NB_DEV), 0, 1 << 20) * NB_DEV + jnp.arange(NB_DEV)[None, :]
    local_order = jnp.argsort(local_scores, axis=1)[:, :NLOC]
    local_ids = device[:, None] * NB_DEV + local_order
    cand_scores = jax.random.randint(key_two, (dom_count, dom_count, NB_DEV), 0, 1 << 20) * NB_DEV + jnp.arange(NB_DEV)[None, None, :]
    chosen = jnp.argsort(cand_scores, axis=2)[:, :, :CAP]
    shift_by = jax.random.randint(key_three, (BLOCKS, NEXP), 1, dom_count)
    source = (device[:, None] + shift_by) % dom_count
    which_one = jax.random.randint(key_four, (BLOCKS, NEXP), 0, CAP)
    forced = (jnp.arange(BLOCKS) % NB_DEV == 0)[:, None] & (jnp.arange(NEXP) < CAP)[None, :]
    source = jnp.where(forced, (device[:, None] + 1) % dom_count, source)
    which_one = jnp.where(forced, jnp.arange(NEXP)[None, :], which_one)
    remote = source * NB_DEV + chosen[device[:, None], source, which_one]
    return jnp.concatenate([local_ids, remote], axis=1).astype(jnp.int32)


def with_spikes(values, key, source, target, shards_of, factor):
    owner, partner = [(jnp.arange(values.shape[axis_at]) // (values.shape[axis_at] // shards_of)).reshape([-1 if axis == axis_at else 1 for axis in range(values.ndim)]) for axis_at in (source, target)]
    chosen = jax.random.permutation(key, shards_of)[partner]
    strong = (owner == chosen) | (owner == (partner + shards_of // 2) % shards_of)
    return jnp.where(strong, factor * values, values)


def block_scale(key, extent, shards, least, high):
    def one(dim, parts):
        draws = jax.random.uniform(jax.random.fold_in(jax.random.fold_in(key, 6), dim), (parts,), jnp.float32, least / len(shards), high / len(shards))
        return jnp.repeat(jnp.exp(draws), extent[dim] // parts).reshape((-1,) + (1,) * (len(extent) - dim - 1))

    gain = one(*shards[0])
    for cut in shards[1:]:
        gain = gain * one(*cut)
    return gain


def noise(stream_key, extent, deviation, reach, pieces=(), held_as=jnp.bfloat16):
    values = deviation * jax.random.normal(stream_key, extent, jnp.float32)
    if pieces:
        values = values * block_scale(stream_key, extent, pieces, -0.22, 0.18)
    return jnp.clip(values, -reach, reach).astype(held_as)


def bell_draw_with(own_key, dims, deviation, limit, shards, heavy, kind=jnp.bfloat16):
    values = deviation * jax.random.normal(own_key, dims, jnp.float32)
    if shards:
        values = values * block_scale(own_key, dims, shards, -0.22, 0.18)
    return jnp.clip(with_spikes(values, jax.random.fold_in(own_key, 3), *heavy), -limit, limit).astype(kind)


def setup_inputs(seed: int = 0) -> dict:
    key_list = jax.random.split(jax.random.key(seed), 8)
    node_feats = draw_node_feats(jax.random.fold_in(key_list[7], 71), 0)
    block_list = draw_block_list(jax.random.fold_in(key_list[7], 71), 0)
    w_query = noise(key_list[2], (MODEL_WIDTH, MODEL_WIDTH), MODEL_WIDTH ** -0.5, 0.1875, ((0, 8), (1, 4)))
    w_key = noise(key_list[3], (MODEL_WIDTH, MODEL_WIDTH), MODEL_WIDTH ** -0.5, 0.1875, ((0, 8), (1, 4)))
    w_value = noise(key_list[4], (MODEL_WIDTH, MODEL_WIDTH), MODEL_WIDTH ** -0.5, 0.1875, ((0, 8), (1, 4)))
    w_out = noise(key_list[5], (MODEL_WIDTH, MODEL_WIDTH), MODEL_WIDTH ** -0.5, 0.1875, ((0, 8), (1, 4)))
    cotangent = bell_draw_with(key_list[6], (NODES, MODEL_WIDTH), 1.0, 6.0, ((0, 8),), (0, 1, 8, 2.0))
    return {"node_feats": node_feats, "block_list": block_list, "w_query": w_query, "w_key": w_key, "w_value": w_value, "w_out": w_out, "cotangent": cotangent}


def block_rows(table, listed_blocks):
    selected_rows = table.reshape(BLOCKS, BLOCK_NODES, MODEL_WIDTH)[listed_blocks]
    return selected_rows.reshape(SLOTS_PER_BLOCK * BLOCK_NODES, HEAD_COUNT, HEAD_WIDTH).astype(jnp.float32)


def probabilities(q_block, k_rows):
    q_heads = q_block.reshape(BLOCK_NODES, HEAD_COUNT, HEAD_WIDTH).astype(jnp.float32)
    scores = jnp.einsum("qhd,khd->hqk", q_heads, k_rows) * (HEAD_WIDTH ** -0.5)
    row_peak = jnp.max(scores, axis=-1, keepdims=True)
    exp_scores = jnp.exp(scores - row_peak)
    return exp_scores / jnp.sum(exp_scores, axis=-1, keepdims=True)


def to_bf(array):
    return lax.optimization_barrier(array.astype(jnp.bfloat16)).astype(jnp.float32)


def grouped_sum(operand_pairs):
    group_cols = MODEL_WIDTH // N_HEAD
    running = jnp.zeros((NODES, MODEL_WIDTH), jnp.float32)
    for group_idx in range(N_HEAD):
        col_low = group_idx * group_cols
        partial_value = jnp.zeros((NODES, MODEL_WIDTH), jnp.float32)
        for activation, weight in operand_pairs:
            partial_value = partial_value + jnp.dot(activation[:, col_low:col_low + group_cols], weight[:, col_low:col_low + group_cols].T, preferred_element_type=jnp.float32)
        running = running + to_bf(partial_value)
    return running


def reference(node_feats, block_list, w_query, w_key, w_value, w_out, cotangent):
    queries = jnp.dot(node_feats, w_query, preferred_element_type=jnp.float32).astype(jnp.bfloat16)
    keys_all = jnp.dot(node_feats, w_key, preferred_element_type=jnp.float32).astype(jnp.bfloat16)
    values_all = jnp.dot(node_feats, w_value, preferred_element_type=jnp.float32).astype(jnp.bfloat16)
    q_blocks = queries.reshape(BLOCKS, BLOCK_NODES, MODEL_WIDTH)

    def attend(inputs):
        q_block, listed_blocks = inputs
        k_rows = block_rows(keys_all, listed_blocks)
        v_rows = block_rows(values_all, listed_blocks)
        rounded = to_bf(probabilities(q_block, k_rows))
        mixed_rows = jnp.einsum("hqk,khd->qhd", rounded, v_rows)
        return mixed_rows.reshape(BLOCK_NODES, MODEL_WIDTH).astype(jnp.bfloat16)

    attended = lax.map(attend, (q_blocks, block_list)).reshape(NODES, MODEL_WIDTH)
    mixed_out = (node_feats.astype(jnp.float32) + grouped_sum([(attended, w_out)])).astype(jnp.bfloat16)

    grad_attended = jnp.dot(cotangent, w_out, preferred_element_type=jnp.float32).astype(jnp.bfloat16)
    g_blocks = grad_attended.reshape(BLOCKS, BLOCK_NODES, MODEL_WIDTH)

    def backward_step(carried, inputs):
        key_accumulator, value_accumulator = carried
        q_block, g_block, listed_blocks = inputs
        k_rows = block_rows(keys_all, listed_blocks)
        v_rows = block_rows(values_all, listed_blocks)
        soft_weights = probabilities(q_block, k_rows)
        rounded = to_bf(soft_weights)
        q_heads = q_block.reshape(BLOCK_NODES, HEAD_COUNT, HEAD_WIDTH).astype(jnp.float32)
        g_heads = g_block.reshape(BLOCK_NODES, HEAD_COUNT, HEAD_WIDTH).astype(jnp.float32)
        gradient_value_copies = jnp.einsum("hqk,qhd->khd", rounded, g_heads)
        grad_probs = jnp.einsum("qhd,khd->hqk", g_heads, v_rows)
        centre = jnp.sum(soft_weights * grad_probs, axis=-1, keepdims=True)
        grad_scores = to_bf(soft_weights * (grad_probs - centre) * (HEAD_WIDTH ** -0.5))
        grad_q = jnp.einsum("hqk,khd->qhd", grad_scores, k_rows).reshape(BLOCK_NODES, MODEL_WIDTH).astype(jnp.bfloat16)
        gradient_key_copies = jnp.einsum("hqk,qhd->khd", grad_scores, q_heads)
        key_accumulator = key_accumulator.at[listed_blocks].add(gradient_key_copies.reshape(SLOTS_PER_BLOCK, BLOCK_NODES, MODEL_WIDTH))
        value_accumulator = value_accumulator.at[listed_blocks].add(gradient_value_copies.reshape(SLOTS_PER_BLOCK, BLOCK_NODES, MODEL_WIDTH))
        return (key_accumulator, value_accumulator), grad_q

    zero_acc = jnp.zeros((BLOCKS, BLOCK_NODES, MODEL_WIDTH), jnp.float32)
    (key_accumulator, value_accumulator), grad_queries = lax.scan(backward_step, (zero_acc, zero_acc), (q_blocks, g_blocks, block_list))
    grad_queries = grad_queries.reshape(NODES, MODEL_WIDTH)
    grad_keys = key_accumulator.reshape(NODES, MODEL_WIDTH).astype(jnp.bfloat16)
    grad_values = value_accumulator.reshape(NODES, MODEL_WIDTH).astype(jnp.bfloat16)
    in_sum = grouped_sum([(grad_queries, w_query), (grad_keys, w_key), (grad_values, w_value)])
    grad_feats = (cotangent.astype(jnp.float32) + in_sum).astype(jnp.bfloat16)
    grad_wq = jnp.dot(node_feats.T, grad_queries, preferred_element_type=jnp.float32)
    grad_wk = jnp.dot(node_feats.T, grad_keys, preferred_element_type=jnp.float32)
    grad_wv = jnp.dot(node_feats.T, grad_values, preferred_element_type=jnp.float32)
    grad_wo = jnp.dot(cotangent.T, attended, preferred_element_type=jnp.float32)
    return mixed_out, grad_feats, grad_wq, grad_wk, grad_wv, grad_wo
```

```python
import functools

import jax
import jax.numpy as jnp
from jax import lax
from jax.experimental import pallas as pl
from jax.experimental.pallas import tpu as pltpu
from jax.sharding import PartitionSpec as P

HEAD_WIDTH = 64
BLOCK_NODES = 128
CAP = 2
PAIR = 2 * HEAD_WIDTH
BF = jnp.bfloat16
F32 = jnp.float32


def nt(a, b):
    return lax.dot_general(a, b, (((1,), (1,)), ((), ())), preferred_element_type=F32)


def tn(a, b):
    return lax.dot_general(a, b, (((0,), (0,)), ((), ())), preferred_element_type=F32)


def nn(a, b):
    return lax.dot_general(a, b, (((1,), (0,)), ((), ())), preferred_element_type=F32)


def grid_of(dom):
    wide = 1
    while 8 * wide * wide <= dom:
        wide *= 2
    return dom // wide, wide


def pack_kernel(pick_ref, feats_ref, *outs):
    for k, out in enumerate(outs):
        for c in range(CAP):
            row = pl.multiple_of(pick_ref[k * CAP + c] * BLOCK_NODES, BLOCK_NODES)
            out[pl.ds(c * BLOCK_NODES, BLOCK_NODES), :] = feats_ref[pl.ds(row, BLOCK_NODES), :]


def pack(picks, head_index, node_feats, quarter, others):
    rows = node_feats.shape[0]
    scalars = jnp.concatenate([picks.reshape(-1), head_index[None]]).astype(jnp.int32)
    last = others * CAP
    block = CAP * BLOCK_NODES
    return pl.pallas_call(
        pack_kernel,
        out_shape=[jax.ShapeDtypeStruct((block, quarter), BF)] * others,
        grid_spec=pltpu.PrefetchScalarGridSpec(
            num_scalar_prefetch=1,
            grid=(1,),
            in_specs=[pl.BlockSpec((rows, quarter), lambda i, s: (0, s[last]))],
            out_specs=[pl.BlockSpec((block, quarter), lambda i, s: (0, 0))] * others,
        ),
        name="pack",
    )(scalars, node_feats)


def project_kernel(n_head, n_piece, own_steps, col_width, scal_ref, *refs):
    feats_ref, cot_ref = refs[:2]
    far_refs = refs[2 : 2 + n_head]
    piece_refs = refs[2 + n_head : 2 + n_head + n_piece]
    all_ref, kv_ref, kvt_ref, q_ref, g_ref, w_ref = refs[2 + n_head + n_piece :]
    step = pl.program_id(0)
    head = scal_ref[0]
    rows = piece_refs[0].shape[0]
    quarter = far_refs[0].shape[1]

    @pl.when(step == 0)
    def _():
        for p in range(n_piece):
            row = pl.multiple_of(scal_ref[1 + p] * rows, rows)
            w_ref[pl.ds(row, rows), :] = piece_refs[p][...]

    @pl.when(step < own_steps)
    def _():
        feats = feats_ref[...]
        all_ref[...] = feats
        query = nn(feats, w_ref[:, 2 * col_width : 3 * col_width]).astype(BF)
        q_ref[...] = (query.astype(F32) * HEAD_WIDTH**-0.5).astype(BF)
        g_ref[...] = nn(cot_ref[...], w_ref[:, 3 * col_width :]).astype(BF)

    @pl.when(step >= own_steps)
    def _():
        for j in range(n_head):
            col = pl.multiple_of((head ^ j) * quarter, quarter)
            all_ref[:, pl.ds(col, quarter)] = far_refs[j][...]

    kv = nn(all_ref[...], w_ref[:, : 2 * col_width])
    kv_ref[...] = kv.astype(BF)
    kvt_ref[...] = kv.T.astype(BF)


def project(node_feats, cotangent, far, pieces, scalars, col_width):
    rows, width = node_feats.shape
    chunk = CAP * BLOCK_NODES
    own_steps = rows // chunk
    steps = own_steps + far[0].shape[0] // chunk
    n_head, n_piece = len(far), len(pieces)
    quarter = far[0].shape[1]
    total = steps * chunk

    def own(i, s):
        return (jnp.minimum(i, own_steps - 1), 0)

    def other(i, s):
        return (jnp.maximum(i - own_steps, 0), 0)

    def fixed(i, s):
        return (0, 0)

    return pl.pallas_call(
        functools.partial(project_kernel, n_head, n_piece, own_steps, col_width),
        out_shape=[
            jax.ShapeDtypeStruct((total, width), BF),
            jax.ShapeDtypeStruct((total, 2 * col_width), BF),
            jax.ShapeDtypeStruct((2 * col_width, total), BF),
            jax.ShapeDtypeStruct((rows, col_width), BF),
            jax.ShapeDtypeStruct((rows, col_width), BF),
            jax.ShapeDtypeStruct((width, 4 * col_width), BF),
        ],
        grid_spec=pltpu.PrefetchScalarGridSpec(
            num_scalar_prefetch=1,
            grid=(steps,),
            in_specs=[pl.BlockSpec((chunk, width), own)] * 2
            + [pl.BlockSpec((chunk, quarter), other)] * n_head
            + [pl.BlockSpec(pieces[0].shape, fixed)] * n_piece,
            out_specs=[
                pl.BlockSpec((chunk, width), lambda i, s: (i, 0)),
                pl.BlockSpec((chunk, 2 * col_width), lambda i, s: (i, 0)),
                pl.BlockSpec((2 * col_width, chunk), lambda i, s: (0, i)),
                pl.BlockSpec((chunk, col_width), own),
                pl.BlockSpec((chunk, col_width), own),
                pl.BlockSpec((width, 4 * col_width), fixed),
            ],
        ),
        cost_estimate=pl.CostEstimate(
            flops=4 * total * width * col_width, bytes_accessed=8 * total * width, transcendentals=0
        ),
        name="project",
    )(scalars, node_feats, cotangent, *far, *pieces)


def attend_kernel(slots, slot_ref, q_ref, g_ref, kv_ref, kvt_ref, att_ref, dq_ref, dkv_ref, ks, vs, kt, vt, acc):
    block = pl.program_id(0)
    col_width = q_ref.shape[1]
    nodes = q_ref.shape[0]

    @pl.when(block == 0)
    def _():
        acc[...] = jnp.zeros_like(acc)

    starts = []
    for s in range(slots):
        start = pl.multiple_of(slot_ref[block * slots + s] * BLOCK_NODES, BLOCK_NODES)
        starts.append(start)
        rows = pl.ds(s * BLOCK_NODES, BLOCK_NODES)
        ks[rows, :] = kv_ref[pl.ds(start, BLOCK_NODES), :col_width]
        vs[rows, :] = kv_ref[pl.ds(start, BLOCK_NODES), col_width:]
        kt[:, rows] = kvt_ref[:col_width, pl.ds(start, BLOCK_NODES)]
        vt[:, rows] = kvt_ref[col_width:, pl.ds(start, BLOCK_NODES)]

    lane = lax.broadcasted_iota(jnp.int32, (nodes, PAIR), 1)
    low = lane < HEAD_WIDTH
    zero = jnp.zeros((nodes, PAIR), BF)
    for t in range(col_width // PAIR):
        cols = slice(t * PAIR, (t + 1) * PAIR)
        q, g = q_ref[:, cols], g_ref[:, cols]
        q_bd = jnp.concatenate([jnp.where(low, q, zero), jnp.where(low, zero, q)], axis=0)
        g_bd = jnp.concatenate([jnp.where(low, g, zero), jnp.where(low, zero, g)], axis=0)
        scores = nt(ks[:, cols], q_bd)
        peak = jnp.max(scores, axis=0, keepdims=True)
        weights = jnp.exp(scores - peak)
        weights = weights * (1.0 / jnp.sum(weights, axis=0, keepdims=True))
        probs = weights.astype(BF)
        attended = nn(vt[cols, :], probs)
        grad_v = nn(probs, g_bd)
        grad_p = nt(vs[:, cols], g_bd)
        centre = jnp.sum(weights * grad_p, axis=0, keepdims=True)
        grad_s = (weights * (grad_p - centre)).astype(BF)
        grad_q = nn(kt[cols, :], grad_s) * HEAD_WIDTH**-0.5
        grad_k = nn(grad_s, q_bd)
        for out, val in ((att_ref, attended), (dq_ref, grad_q)):
            diag = jnp.concatenate([val[:HEAD_WIDTH, :nodes], val[HEAD_WIDTH:, nodes:]], axis=0)
            out[:, cols] = diag.T.astype(BF)
        vcols = slice(col_width + t * PAIR, col_width + (t + 1) * PAIR)
        for s in range(slots):
            part = slice(s * BLOCK_NODES, (s + 1) * BLOCK_NODES)
            acc[pl.ds(starts[s], BLOCK_NODES), cols] += grad_k[part]
            acc[pl.ds(starts[s], BLOCK_NODES), vcols] += grad_v[part]

    @pl.when(block == pl.num_programs(0) - 1)
    def _():
        dkv_ref[...] = acc[...].astype(BF)


def attend(slot_rows, queries, grads, kv, kvt):
    blocks, slots = slot_rows.shape
    rows, col_width = queries.shape
    total = kv.shape[0]
    span = slots * BLOCK_NODES

    def mine(i, s):
        return (i, 0)

    def fixed(i, s):
        return (0, 0)

    return pl.pallas_call(
        functools.partial(attend_kernel, slots),
        out_shape=[
            jax.ShapeDtypeStruct((rows, col_width), BF),
            jax.ShapeDtypeStruct((rows, col_width), BF),
            jax.ShapeDtypeStruct((total, 2 * col_width), BF),
        ],
        grid_spec=pltpu.PrefetchScalarGridSpec(
            num_scalar_prefetch=1,
            grid=(blocks,),
            in_specs=[
                pl.BlockSpec((BLOCK_NODES, col_width), mine),
                pl.BlockSpec((BLOCK_NODES, col_width), mine),
                pl.BlockSpec((total, 2 * col_width), fixed),
                pl.BlockSpec((2 * col_width, total), fixed),
            ],
            out_specs=[
                pl.BlockSpec((BLOCK_NODES, col_width), mine),
                pl.BlockSpec((BLOCK_NODES, col_width), mine),
                pl.BlockSpec((total, 2 * col_width), fixed),
            ],
            scratch_shapes=[
                pltpu.VMEM((span, col_width), BF),
                pltpu.VMEM((span, col_width), BF),
                pltpu.VMEM((col_width, span), BF),
                pltpu.VMEM((col_width, span), BF),
                pltpu.VMEM((total, 2 * col_width), F32),
            ],
        ),
        cost_estimate=pl.CostEstimate(
            flops=24 * rows * span * col_width, bytes_accessed=6 * total * col_width, transcendentals=rows * span * 4
        ),
        name="attend",
    )(slot_rows.reshape(-1), queries, grads, kv, kvt)


def combine_kernel(pick_ref, base_ref, *refs):
    arrivals, out_ref, acc = refs[:-2], refs[-2], refs[-1]
    acc[...] = base_ref[...]
    for k, got in enumerate(arrivals):
        for c in range(CAP):
            row = pl.multiple_of(pick_ref[k * CAP + c] * BLOCK_NODES, BLOCK_NODES)
            acc[pl.ds(row, BLOCK_NODES), :] += got[pl.ds(c * BLOCK_NODES, BLOCK_NODES), :].astype(F32)
    out_ref[...] = acc[...].astype(BF)


def combine(picks, base, arrivals):
    return pl.pallas_call(
        combine_kernel,
        out_shape=jax.ShapeDtypeStruct(base.shape, BF),
        grid_spec=pltpu.PrefetchScalarGridSpec(
            num_scalar_prefetch=1,
            grid=(1,),
            in_specs=[pl.BlockSpec(a.shape, lambda i, s: (0, 0)) for a in (base, *arrivals)],
            out_specs=pl.BlockSpec(base.shape, lambda i, s: (0, 0)),
            scratch_shapes=[pltpu.VMEM(base.shape, F32)],
        ),
        name="combine",
    )(picks.reshape(-1), base, *arrivals)


def body(dom, n_head, node_feats, block_list, w_query, w_key, w_value, w_out, cotangent):
    rows, width = node_feats.shape
    me = lax.axis_index("dom")
    head = lax.axis_index("head")
    nb = rows // BLOCK_NODES
    slots = block_list.shape[1]
    col_width = w_query.shape[1]
    shard = w_query.shape[0]
    quarter = width // n_head
    deep, wide = grid_of(dom)
    my_z, my_y = me // wide, me % wide
    others = dom - 1
    half = CAP * BLOCK_NODES

    def rotate(x, k):
        return lax.ppermute(x, "dom", [(i, (i + k) % dom) for i in range(dom)])

    def turn_z(x, k):
        return lax.ppermute(x, "dom", [(i, (i + k * wide) % dom) for i in range(dom)])

    def turn_y(x, k):
        return lax.ppermute(x, "dom", [(i, i - i % wide + (i + k) % wide) for i in range(dom)])

    def swap(x, bit):
        return lax.ppermute(x, "head", [(i, i ^ bit) for i in range(n_head)])

    part = block_list // nb
    by_part = part.reshape(dom, nb * slots)
    local = block_list.reshape(dom, nb * slots) - me * nb
    first = jnp.min(jnp.where(by_part == me, local, nb - 1), axis=1)
    second = jnp.max(jnp.where(by_part == me, local, 0), axis=1)
    dests = (me + 1 + jnp.arange(others)) % dom
    picks = jnp.stack([first[dests], second[dests]], axis=1).astype(jnp.int32)

    my_ids = lax.dynamic_slice_in_dim(block_list, me * nb, nb, 0)
    my_part = my_ids // nb
    hot = my_part[:, :, None] == jnp.arange(dom)[None, None, :]
    least = jnp.min(jnp.where(hot, my_ids[:, :, None], nb * dom), axis=(0, 1))
    my_least = jnp.sum(jnp.where(hot, least[None, None, :], 0), axis=2)
    away = nb + ((me - my_part) % dom - 1) * CAP + (my_ids != my_least)
    slot_rows = jnp.where(my_part == me, my_ids - me * nb, away).astype(jnp.int32)

    sends = pack(picks, head, node_feats, quarter, others)
    got = [rotate(sends[k], k + 1) for k in range(others)]

    mine = jnp.concatenate([w_key, w_value, w_query, w_out], axis=1)
    along = [mine] + [turn_z(mine, k) for k in range(1, deep)]
    pieces = list(along)
    places = [((my_z - k) % deep) * wide + my_y for k in range(deep)]
    for j in range(1, wide):
        for k in range(deep):
            pieces.append(turn_y(along[k], j))
            places.append(((my_z - k) % deep) * wide + (my_y - j) % wide)

    groups = {0: got}
    bit = n_head // 2
    while bit > 1:
        for j in list(groups):
            groups[j ^ bit] = [swap(x, bit) for x in groups[j]]
        bit //= 2
    far = {j: jnp.concatenate(g, axis=0) for j, g in groups.items()}
    for j in list(far):
        far[j ^ 1] = swap(far[j], 1)
    far = [far[j] for j in range(n_head)]

    scalars = jnp.stack([head] + places).astype(jnp.int32)
    all_feats, kv, kvt, queries, grads, weights = project(
        node_feats, cotangent, far, pieces, scalars, col_width
    )
    attended, grad_q, grad_kv = attend(slot_rows, queries, grads, kv, kvt)

    own_kvq = jnp.concatenate([grad_kv[:rows], grad_q], axis=1)
    far_kv = grad_kv[rows:]
    near, away_part = [], []
    for j in range(n_head):
        w_rows = lax.dynamic_slice_in_dim(weights, (head ^ j) * quarter, quarter, 0)
        away_part.append(nt(far_kv, w_rows[:, : 2 * col_width]).astype(BF))
        own_in = nt(own_kvq, w_rows[:, : 3 * col_width]).astype(BF)
        own_out = nt(attended, w_rows[:, 3 * col_width :]).astype(BF)
        near.append(jnp.concatenate([own_out, own_in], axis=0))

    def head_sum(parts):
        bit = 1
        while bit < n_head:
            last = 2 * bit >= n_head
            for j in range(0, n_head, 2 * bit):
                total = parts[j].astype(F32) + swap(parts[j + bit], bit).astype(F32)
                parts[j] = total if last else total.astype(BF)
            bit *= 2
        return parts[0]

    away_sum = head_sum(away_part).astype(BF)
    near_sum = head_sum(near)
    back = [rotate(away_sum[k * half : (k + 1) * half], -(k + 1)) for k in range(others)]

    col = head * quarter
    own_feats = lax.dynamic_slice_in_dim(node_feats, col, quarter, 1).astype(F32)
    own_cot = lax.dynamic_slice_in_dim(cotangent, col, quarter, 1).astype(F32)
    mixed_out = (own_feats + near_sum[:rows]).astype(BF)
    grad_feats = combine(picks, own_cot + near_sum[rows:], back)

    grad_w = jnp.concatenate(
        [
            tn(all_feats, grad_kv).astype(BF),
            tn(node_feats, grad_q).astype(BF),
            tn(cotangent, attended).astype(BF),
        ],
        axis=1,
    ).reshape(deep, wide, shard, 4 * col_width)

    def slab_y(j):
        return lax.dynamic_index_in_dim(grad_w, (my_y + j) % wide, 1, keepdims=False)

    col_sum = slab_y(0).astype(F32)
    for j in range(1, wide):
        col_sum = col_sum + turn_y(slab_y(j), j).astype(F32)
    col_bf = col_sum.astype(BF)
    total = lax.dynamic_index_in_dim(col_sum, my_z, 0, keepdims=False)
    for k in range(1, deep):
        piece = lax.dynamic_index_in_dim(col_bf, (my_z + k) % deep, 0, keepdims=False)
        total = total + turn_z(piece, k).astype(F32)
    grad_wk, grad_wv, grad_wq, grad_wo = (
        total[:, i * col_width : (i + 1) * col_width] for i in range(4)
    )
    return (mixed_out, grad_feats, grad_wq, grad_wk, grad_wv, grad_wo)


def solution(mesh):
    rows, both = P("dom", None), P("dom", "head")
    return jax.shard_map(
        functools.partial(body, mesh.shape["dom"], mesh.shape["head"]),
        mesh=mesh,
        in_specs=(rows, P(), both, both, both, both, rows),
        out_specs=(both,) * 6,
        check_vma=False,
    )
```
